512 devices in a mesh: cp: 64 (over x, y, core), dp: 8 (over z).
Axes of the slice: x: 4, y: 8, z: 8, core: 2. Of those that a mesh axis runs over, the one named last changes fastest.
Arguments:
- queries: bfloat16 [65536, 4096], P(('dp', 'cp')), parts along dimension 0, may hold values from -200 to 200
- keys: bfloat16 [65536, 512], P(('dp', 'cp')), parts along dimension 0, may hold values from -6 to 6
- values: bfloat16 [65536, 512], P(('dp', 'cp')), parts along dimension 0, may hold values from -6 to 6
- segments: int32 [65536], P('dp'), parts along dimension 0, may hold values from 0 to 15, never falling along the last dimension, each value on 1 to 1024 neighbouring positions
- loss_mask: int32 [65536], P(('dp', 'cp')), parts along dimension 0, may hold values 0 or 1
- grad_out: bfloat16 [65536, 4096], P(('dp', 'cp')), parts along dimension 0, may hold values from -6 to 6
Outputs:
- grad_q: bfloat16 [65536, 4096], P(('dp', 'cp')), parts along dimension 0
- grad_k: bfloat16 [65536, 512], P(('dp', 'cp')), parts along dimension 0
- grad_v: bfloat16 [65536, 512], P(('dp', 'cp')), parts along dimension 0
The draws below stay inside these ranges and needn't reach their ends.
There are 8 independent parts, one for each index of `dp`. The reference program is written for one: setup_inputs(seed, part) draws one part's arguments, and reference() takes and returns one part's arrays. A program takes and returns all parts, laid end to end along the dimension named above; each array names one. Nothing has to cross between parts.
Inputs may be any that keep to these rules, and one draw needn't show every extreme that they name: `segments`: document ids never fall along the sequence; every document holds 1 to 1024 tokens and one holds exactly 1024.
All inputs are finite; a program needn't handle non-finite values. No bound on the sum of `loss_mask` on one device may be relied on, other than what follows from the above.
Results may differ from the reference program's by a relative error of at most 0.019.
Values may be sent and summed in bfloat16 or wider, within the bound.
A program may use at most 64 MiB of HBM per device.

```python
import math
import jax
import jax.numpy as jnp
import numpy as np
from jax import lax

QH = 32
KVH = 4
HD = 128
TOK_DEV = 128
RADIUS = 8
SEQ = 8192
DOC_MOST = 1024
DOCS = 16


def shared_keys(key):
    base = jax.random.normal(jax.random.fold_in(key, 11), (SEQ, KVH * HD), jnp.float32)
    base = jnp.clip(base, -5.5, 5.5)
    return base


def draw_keys(key, part):
    return shared_keys(key).astype(jnp.bfloat16)


def draw_queries(key, part):
    drawn = jax.random.normal(jax.random.fold_in(key, 21), (SEQ, QH * HD), jnp.float32)
    drawn = jnp.clip(drawn, -6.0, 6.0)
    return drawn.astype(jnp.bfloat16)


def set_ends(entries, own_key, low, largest):
    dims = entries.shape
    spot = [jax.random.randint(jax.random.fold_in(own_key, axis), (), 0, dims[axis]) for axis in range(len(dims))]
    entries = entries.at[tuple(spot)].set(low)
    longest = dims.index(max(dims))
    spot[longest] = (spot[longest] + 1) % dims[longest]
    return entries.at[tuple(spot)].set(largest)


def steps_of(stream_key, shape, shards, smallest, top_value):
    def one(position, parts):
        steps = jax.random.uniform(jax.random.fold_in(jax.random.fold_in(stream_key, 6), position), (parts,), jnp.float32, smallest / len(shards), top_value / len(shards))
        return jnp.repeat(jnp.exp(steps), shape[position] // parts).reshape((-1,) + (1,) * (len(shape) - position - 1))

    gain = one(*shards[0])
    for cut in shards[1:]:
        gain = gain * one(*cut)
    return gain


def length_profile(count, total, most, lean):
    weights = [(1 << 20) // math.isqrt(grade ** lean) + 1 for grade in range(2, count + 1)]
    rest, holding = total - most - (count - 1), [1] * (count - 1)
    while rest > 0:
        free = [i for i in range(count - 1) if holding[i] < most]
        whole, remaining = sum([weights[i] for i in free]), rest
        for i in free:
            more = min(most - holding[i], max(1, remaining * weights[i] // whole), rest)
            holding[i] = holding[i] + more
            rest = rest - more
    return np.array([most] + holding)


def uneven(stream_key, amount, total, reach, skew):
    if amount == 2:
        one = jax.random.randint(stream_key, (), max(1, total - reach), min(reach, total - 1) + 1)
        return jnp.stack([one, total - one])
    tallies = jnp.asarray(length_profile(amount, total, reach, skew), jnp.int32)
    couples = (amount - 1) // 2
    giver, taker = tallies[1:1 + 2 * couples:2], tallies[2:2 + 2 * couples:2]
    room = jnp.minimum(giver - 1, reach - taker)
    passed = jax.random.randint(jax.random.fold_in(stream_key, 1), (couples,), 0, 1 << 20) % (room + 1)
    tallies = tallies.at[1:1 + 2 * couples:2].set(giver - passed).at[2:2 + 2 * couples:2].set(taker + passed)
    return tallies[jax.random.permutation(jax.random.fold_in(stream_key, 2), amount)]


def gaussian(stream_key, extent, width, reach, shards=(), held_as=jnp.bfloat16):
    gain = steps_of(stream_key, extent, shards, -0.22, 0.18) if shards else 1.0
    entries = jax.random.normal(stream_key, extent, jnp.float32) * width * gain
    return jnp.minimum(jnp.maximum(entries, -reach), reach).astype(held_as)


def setup_inputs(seed: int = 0, part: int = 0) -> dict:
    arg_keys = jax.random.split(jax.random.key(seed), 7)
    part_splits = jax.random.split(jax.random.fold_in(arg_keys[6], part), 7)
    return {
        "queries": draw_queries(jax.random.fold_in(jax.random.fold_in(arg_keys[6], part), 71), part),
        "keys": draw_keys(jax.random.fold_in(jax.random.fold_in(arg_keys[6], part), 71), part),
        "values": gaussian(part_splits[2], (SEQ, KVH * HD), 1.0, 6.0, ((0, 64),)),
        "segments": jnp.searchsorted(jnp.cumsum(uneven(part_splits[3], DOCS, SEQ, DOC_MOST, 1)), jnp.arange(SEQ), side="right").astype(jnp.int32),
        "loss_mask": set_ends((jax.random.randint(part_splits[4], (SEQ,), 0, 4) < 3).astype(jnp.int32), jax.random.fold_in(part_splits[4], 1), 0, 1),
        "grad_out": gaussian(part_splits[5], (SEQ, QH * HD), 1.0, 6.0, ((0, 64),)),
    }


def reference(queries, keys, values, segments, loss_mask, grad_out):
    rows = TOK_DEV
    span = (RADIUS + 1) * rows
    lead = RADIUS * rows
    group = QH // KVH
    scale = HD ** -0.5
    kv_width = KVH * HD
    key_pad = jnp.concatenate([jnp.zeros((lead, kv_width), jnp.bfloat16), keys], 0)
    val_pad = jnp.concatenate([jnp.zeros((lead, kv_width), jnp.bfloat16), values], 0)
    seg_pad = jnp.concatenate([jnp.full((lead,), -1, jnp.int32), segments.astype(jnp.int32)], 0)
    masked = grad_out * loss_mask[:, None].astype(jnp.bfloat16)

    def block(carry, index):
        grad_keys, grad_vals = carry
        start = (index * rows).astype(jnp.int32)
        q_part = lax.dynamic_slice_in_dim(queries, start, rows, 0).astype(jnp.float32).reshape(rows, KVH, group, HD)
        o_part = lax.dynamic_slice_in_dim(masked, start, rows, 0).astype(jnp.float32).reshape(rows, KVH, group, HD)
        k_part = lax.dynamic_slice_in_dim(key_pad, start, span, 0).astype(jnp.float32).reshape(span, KVH, HD)
        v_part = lax.dynamic_slice_in_dim(val_pad, start, span, 0).astype(jnp.float32).reshape(span, KVH, HD)
        q_seg = lax.dynamic_slice_in_dim(segments.astype(jnp.int32), start, rows, 0)
        k_seg = lax.dynamic_slice_in_dim(seg_pad, start, span, 0)
        q_pos = start + jnp.arange(rows, dtype=jnp.int32)
        k_pos = start - lead + jnp.arange(span, dtype=jnp.int32)
        allowed = (q_seg[:, None] == k_seg[None, :]) & (k_pos[None, :] <= q_pos[:, None])
        scores = jnp.einsum('tngd,knd->ngtk', q_part, k_part) * scale
        scores = jnp.where(allowed[None, None], scores, -1e30)
        peak = jnp.max(scores, axis=-1, keepdims=True)
        expo = jnp.exp(scores - peak)
        probs = expo / jnp.sum(expo, axis=-1, keepdims=True)
        probs_b = lax.optimization_barrier(probs.astype(jnp.bfloat16)).astype(jnp.float32)
        attended = jnp.einsum('ngtk,knd->tngd', probs_b, v_part).astype(jnp.bfloat16)
        delta = jnp.sum(o_part * attended.astype(jnp.float32), axis=-1)
        dprobs = jnp.einsum('tngd,knd->ngtk', o_part, v_part)
        dscores = probs * (dprobs - jnp.transpose(delta, (1, 2, 0))[..., None])
        dscores = lax.optimization_barrier(dscores.astype(jnp.bfloat16)).astype(jnp.float32)
        dq = (jnp.einsum('ngtk,knd->tngd', dscores, k_part) * scale).astype(jnp.bfloat16)
        dk = jnp.einsum('ngtk,tngd->knd', dscores, q_part) * scale
        dv = jnp.einsum('ngtk,tngd->knd', probs_b, o_part)
        old_k = lax.dynamic_slice_in_dim(grad_keys, start, span, 0)
        old_v = lax.dynamic_slice_in_dim(grad_vals, start, span, 0)
        grad_keys = lax.dynamic_update_slice_in_dim(grad_keys, old_k + dk.reshape(span, kv_width), start, 0)
        grad_vals = lax.dynamic_update_slice_in_dim(grad_vals, old_v + dv.reshape(span, kv_width), start, 0)
        return (grad_keys, grad_vals), dq.reshape(rows, QH * HD)

    total = lead + SEQ
    init = (jnp.zeros((total, kv_width), jnp.float32), jnp.zeros((total, kv_width), jnp.float32))
    (grad_keys, grad_vals), dq_blocks = lax.scan(block, init, jnp.arange(SEQ // rows, dtype=jnp.int32))
    grad_q = dq_blocks.reshape(SEQ, QH * HD)
    grad_k = grad_keys[lead:].astype(jnp.bfloat16)
    grad_v = grad_vals[lead:].astype(jnp.bfloat16)
    return (grad_q, grad_k, grad_v)
```

```python
import functools
import math

import jax
import jax.numpy as jnp
from jax import lax
from jax.experimental import pallas as pl
from jax.experimental.pallas import tpu as pltpu
from jax.sharding import PartitionSpec as P

HD = 128
BT = 256
ND = 5
G = 8
FAR = ND - 1
NEG = -1e30
F32 = jnp.float32
BF16 = jnp.bfloat16
MESH = pl.DeviceIdType.MESH


def dot(a, b, ca, cb):
    return lax.dot_general(
        a, b, (((ca,), (cb,)), ((), ())), preferred_element_type=F32
    )


def kernel(
    chips, q_hbm, k_hbm, v_hbm, seg_ref, mask_ref, do_hbm,
    dq_out, gk_out, gv_out,
    q_s, o_s, kv_s, bias_s, e_s, dp_s, ds_s, p_s, kt_s, m_s, l_s, dl_s,
    rbuf, sbuf, gacc, gout, dq_s, mk_s,
    f_recv, f_own, f_relay, f_xsend, f_loc,
    q_recv, q_send, q_loc, k_recv, k_send,
    b_recv, b_send, dq_recv, dq_send, dq_loc, g_recv, g_send, g_loc,
):
    me = lax.axis_index("cp")
    core = me % 2
    chip = me // 2
    other = 1 - core
    partner = chip * 2 + other
    after = (chip + 1) % chips
    before = (chip + chips - 1) % chips
    scale = HD ** -0.5
    mine = pl.ds(pl.multiple_of(core * 128, 128), 128)
    theirs = pl.ds(pl.multiple_of(other * 128, 128), 128)

    barrier = pltpu.get_barrier_semaphore()
    for peer in (partner, after * 2, after * 2 + 1, before * 2, before * 2 + 1):
        pl.semaphore_signal(barrier, inc=1, device_id={"cp": peer}, device_id_type=MESH)
    pl.semaphore_wait(barrier, 5)

    def remote(src, dst, ssem, rsem, cp):
        return pltpu.make_async_remote_copy(
            src_ref=src, dst_ref=dst, send_sem=ssem, recv_sem=rsem,
            device_id={"cp": cp}, device_id_type=MESH,
        )

    def columns(first, count=1):
        return pl.ds(pl.multiple_of(first * 128, 128), count * 128)

    srcs = (k_hbm, v_hbm)

    def own_send(hl, kv, b):
        return remote(
            srcs[kv].at[:, columns(2 * b + hl)], kv_s.at[hl, kv, 1, mine, :],
            f_own.at[hl, kv, b], f_recv.at[hl, kv, 1, core], after * 2 + b,
        )

    def x_send(hl, kv):
        return remote(
            srcs[kv].at[:, columns(2 * other + hl)], kv_s.at[hl, kv, 0, mine, :],
            f_xsend.at[hl, kv], f_recv.at[hl, kv, 0, core], partner,
        )

    def x_recv(hl, kv):
        return remote(
            srcs[kv].at[:, columns(2 * other + hl)], kv_s.at[hl, kv, 0, theirs, :],
            f_xsend.at[hl, kv], f_recv.at[hl, kv, 0, other], partner,
        )

    def local_kv(hl, kv):
        return pltpu.make_async_copy(
            srcs[kv].at[:, columns(2 * core + hl)], kv_s.at[hl, kv, 0, mine, :],
            f_loc.at[hl, kv],
        )

    def half(i):
        return pl.ds(i * 128, 128)

    def hop(hl, kv, d, i):
        return remote(
            kv_s.at[hl, kv, d, half(i), :], kv_s.at[hl, kv, d + 1, half(i), :],
            f_relay.at[hl, kv, d - 1, i], f_recv.at[hl, kv, d + 1, i],
            after * 2 + core,
        )

    def hop_recv(hl, kv, d, i):
        return remote(
            kv_s.at[hl, kv, d, half(i), :], kv_s.at[hl, kv, d, half(i), :],
            f_relay.at[hl, kv, 0, i], f_recv.at[hl, kv, d, i],
            after * 2 + core,
        )

    heads = (q_hbm, do_hbm)
    held = (q_s, o_s)

    def qo_send(t, i):
        hl = i // G
        return remote(
            heads[t].at[:, columns(other * 16 + i)], held[t].at[i, mine, :],
            q_send.at[t, hl], q_recv.at[t, hl], partner,
        )

    def qo_local(t, i):
        return pltpu.make_async_copy(
            heads[t].at[:, columns(core * 16 + i)], held[t].at[i, mine, :],
            q_loc.at[t, i // G],
        )

    def qo_wait(t, hl):
        rows = held[t].at[hl * G:(hl + 1) * G, theirs, :]
        remote(rows, rows, q_send.at[t, hl], q_recv.at[t, hl], partner).wait_recv()
        own = held[t].at[hl * G:(hl + 1) * G, mine, :]
        pltpu.make_async_copy(own, own, q_loc.at[t, hl]).wait()

    def qo_wait_send(t, hl):
        rows = held[t].at[hl * G:(hl + 1) * G, theirs, :]
        remote(rows, rows, q_send.at[t, hl], q_recv.at[t, hl], partner).wait_send()

    mask_copy = remote(mask_ref, mk_s.at[core], k_send, k_recv, partner)
    mask_back = remote(mask_ref, mk_s.at[other], k_send, k_recv, partner)

    for kv in range(2):
        for b in range(2):
            own_send(0, kv, b).start()
    for kv in range(2):
        x_send(0, kv).start()
        local_kv(0, kv).start()
    mask_copy.start()
    for t in range(2):
        for i in range(G):
            qo_send(t, i).start()
            qo_local(t, i).start()

    first = 2 * chip - 2 * FAR

    def seg_row(j):
        return seg_ref[pl.ds((first + j + 2 * chips) % (2 * chips), 1), :].astype(F32)

    q_seg = jnp.concatenate([seg_row(2 * FAR), seg_row(2 * FAR + 1)], axis=1)
    q_at = lax.broadcasted_iota(jnp.int32, (128, BT), 1)
    k_at = lax.broadcasted_iota(jnp.int32, (128, BT), 0)
    for j in range(2 * ND):
        row = jnp.broadcast_to(seg_row(j), (128, 128))
        col = jnp.concatenate([row.T] * 2, axis=1)
        offset = (j - 2 * FAR) * 128
        ok = (col == q_seg) & (k_at + offset <= q_at) & (k_at + (first + j) * 128 >= 0)
        bias_s[FAR - j // 2, (j % 2) * 128:(j % 2) * 128 + 128, :] = jnp.where(ok, 0.0, NEG)

    mk_s[pl.ds(core, 1), :, :] = mask_ref[...][None]
    mask_back.wait_recv()
    mask_col = jnp.concatenate(
        [jnp.broadcast_to(mk_s[i].astype(F32), (128, 128)).T for i in range(2)], axis=0
    ).astype(BF16)

    def mask_grad(hl):
        def body(i, carry):
            o_s[hl * G + i] = o_s[hl * G + i] * mask_col
            return carry
        lax.fori_loop(0, G, body, 0)

    def arrive(hl, d):
        for kv in range(2):
            if d == 0:
                local_kv(hl, kv).wait()
                x_recv(hl, kv).wait_recv()
            else:
                for i in range(2):
                    hop_recv(hl, kv, d, i).wait_recv()
                    if d < FAR:
                        hop(hl, kv, d, i).start()

    c2 = scale * math.log2(math.e)

    def pass1(hl, d):
        def body(g, carry):
            s = dot(kv_s[hl, 0, d], q_s[hl * G + g], 1, 1)
            dp = dot(kv_s[hl, 1, d], o_s[hl * G + g], 1, 1)
            x = s * c2 + bias_s[d]
            peak = jnp.max(x, axis=0, keepdims=True)
            if d > 0:
                old = m_s[d - 1, g]
                peak = jnp.maximum(old, peak)
            e = jnp.exp2(x - peak)
            total = jnp.sum(e, axis=0, keepdims=True)
            inner = jnp.sum(e * dp, axis=0, keepdims=True)
            if d > 0:
                fade = jnp.exp2(old - peak)
                total = total + l_s[g] * fade
                inner = inner + dl_s[g] * fade
            m_s[d, g] = peak
            l_s[g] = total
            dl_s[g] = inner
            e_s[g, d] = e
            dp_s[g, d] = dp
            return carry
        lax.fori_loop(0, G, body, 0)

    def pass2(hl, d):
        def body(g, carry):
            inv = 1.0 / l_s[g]
            f = jnp.exp2(m_s[d, g] - m_s[FAR, g]) * inv
            delta = dl_s[g] * inv
            p = e_s[g, d] * f
            p_s[g] = p.astype(BF16)
            ds_s[g, d * BT:(d + 1) * BT, :] = (p * (dp_s[g, d] - delta)).astype(BF16)
            return carry
        lax.fori_loop(0, G, body, 0)
        span = slice(hl * G, (hl + 1) * G)
        ds = jnp.concatenate([ds_s[g, d * BT:(d + 1) * BT, :] for g in range(G)], axis=1)
        gacc[hl, 0, d] = dot(ds, q_s[span].reshape(G * BT, HD), 1, 0)
        p = jnp.concatenate([p_s[g] for g in range(G)], axis=1)
        gacc[hl, 1, d] = dot(p, o_s[span].reshape(G * BT, HD), 1, 0)

    def transposed_keys(hl):
        for d in range(ND):
            kt_s[:, d * BT:(d + 1) * BT] = kv_s[hl, 0, d].astype(F32).T.astype(BF16)

    def grad_q(hl):
        def body(g, carry):
            dqt = dot(kt_s[...], ds_s[g], 1, 0) * scale
            dq_s[:, columns(hl * G + g)] = dqt.T.astype(BF16)
            return carry
        lax.fori_loop(0, G, body, 0)

    def dq_copy(hl):
        return pltpu.make_async_copy(
            dq_s.at[mine, columns(hl * G, G)],
            dq_out.at[:, columns(core * 16 + hl * G, G)], dq_loc.at[hl],
        )

    def dq_give(hl):
        return remote(
            dq_s.at[theirs, columns(hl * G, G)],
            dq_out.at[:, columns(core * 16 + hl * G, G)],
            dq_send.at[hl], dq_recv.at[hl], partner,
        )

    def dq_take(hl):
        return remote(
            dq_s.at[theirs, columns(hl * G, G)],
            dq_out.at[:, columns(other * 16 + hl * G, G)],
            dq_send.at[hl], dq_recv.at[hl], partner,
        )

    def back(hl, kv, d, i):
        return remote(
            sbuf.at[hl, kv, d - 1, half(i), :], rbuf.at[hl, kv, d - 1, half(i), :],
            b_send.at[hl, kv, d - 1, i], b_recv.at[hl, kv, d - 1, i],
            before * 2 + core,
        )

    outs = (gk_out, gv_out)

    def g_copy(hl, kv):
        return pltpu.make_async_copy(
            gout.at[hl, kv, mine, :], outs[kv].at[:, columns(2 * core + hl)],
            g_loc.at[hl, kv],
        )

    def g_give(hl, kv):
        return remote(
            gout.at[hl, kv, theirs, :], outs[kv].at[:, columns(2 * core + hl)],
            g_send.at[hl, kv], g_recv.at[hl, kv], partner,
        )

    def g_take(hl, kv):
        return remote(
            gout.at[hl, kv, theirs, :], outs[kv].at[:, columns(2 * other + hl)],
            g_send.at[hl, kv], g_recv.at[hl, kv], partner,
        )

    def chain(hl, d):
        for kv in range(2):
            for i in range(2):
                rows = slice(i * 128, i * 128 + 128)
                part = gacc[hl, kv, d, rows, :]
                if d < FAR:
                    back(hl, kv, d + 1, i).wait_recv()
                    part = part + rbuf[hl, kv, d, rows, :].astype(F32)
                if d > 0:
                    sbuf[hl, kv, d - 1, rows, :] = part.astype(BF16)
                    back(hl, kv, d, i).start()
                else:
                    if kv == 0:
                        part = part * scale
                    gout[hl, kv, rows, :] = part.astype(BF16)
            if d == 0:
                g_give(hl, kv).start()
                g_copy(hl, kv).start()

    def start_second():
        for kv in range(2):
            for b in range(2):
                own_send(1, kv, b).start()
        for kv in range(2):
            x_send(1, kv).start()
            local_kv(1, kv).start()
        for t in range(2):
            for i in range(G, 2 * G):
                qo_send(t, i).start()
                qo_local(t, i).start()

    qo_wait(0, 0)
    qo_wait(1, 0)
    mask_grad(0)
    for d in range(ND):
        arrive(0, d)
        if d == FAR - 1:
            start_second()
        pass1(0, d)
    pass2(0, 4)
    chain(0, 4)
    arrive(1, 0)
    arrive(1, 1)
    pass2(0, 3)
    pass2(0, 2)
    arrive(1, 2)
    chain(0, 3)
    pass2(0, 1)
    pass2(0, 0)
    arrive(1, 3)
    chain(0, 2)
    transposed_keys(0)
    grad_q(0)
    dq_give(0).start()
    dq_copy(0).start()
    qo_wait(0, 1)
    qo_wait(1, 1)
    mask_grad(1)
    pass1(1, 0)
    chain(0, 1)
    pass1(1, 1)
    pass1(1, 2)
    chain(0, 0)
    pass1(1, 3)
    arrive(1, 4)
    pass1(1, 4)
    pass2(1, 4)
    chain(1, 4)
    pass2(1, 3)
    pass2(1, 2)
    chain(1, 3)
    pass2(1, 1)
    pass2(1, 0)
    chain(1, 2)
    transposed_keys(1)
    grad_q(1)
    dq_give(1).start()
    dq_copy(1).start()
    chain(1, 1)
    chain(1, 0)

    mask_copy.wait_send()
    for hl in range(2):
        for t in range(2):
            qo_wait_send(t, hl)
        dq_give(hl).wait_send()
        dq_copy(hl).wait()
        for kv in range(2):
            for b in range(2):
                own_send(hl, kv, b).wait_send()
            x_send(hl, kv).wait_send()
            for i in range(2):
                for d in range(1, FAR):
                    hop(hl, kv, d, i).wait_send()
                for d in range(1, ND):
                    back(hl, kv, d, i).wait_send()
            g_give(hl, kv).wait_send()
            g_copy(hl, kv).wait()
    for hl in range(2):
        dq_take(hl).wait_recv()
        for kv in range(2):
            g_take(hl, kv).wait_recv()


def per_device(queries, keys, values, segments, loss_mask, grad_out):
    devices = lax.axis_size("cp")
    chips = devices // 2
    dma = pltpu.SemaphoreType.DMA
    anywhere = pl.BlockSpec(memory_space=pl.ANY)
    vmem = pl.BlockSpec(memory_space=pltpu.VMEM)
    return pl.pallas_call(
        functools.partial(kernel, chips),
        out_shape=(
            jax.ShapeDtypeStruct(queries.shape, BF16),
            jax.ShapeDtypeStruct(keys.shape, BF16),
            jax.ShapeDtypeStruct(values.shape, BF16),
        ),
        in_specs=[anywhere, anywhere, anywhere, vmem, vmem, anywhere],
        out_specs=(anywhere, anywhere, anywhere),
        scratch_shapes=[
            pltpu.VMEM((2 * G, BT, HD), BF16),
            pltpu.VMEM((2 * G, BT, HD), BF16),
            pltpu.VMEM((2, 2, ND, BT, HD), BF16),
            pltpu.VMEM((ND, BT, BT), F32),
            pltpu.VMEM((G, ND, BT, BT), F32),
            pltpu.VMEM((G, ND, BT, BT), F32),
            pltpu.VMEM((G, ND * BT, BT), BF16),
            pltpu.VMEM((G, BT, BT), BF16),
            pltpu.VMEM((HD, ND * BT), BF16),
            pltpu.VMEM((ND, G, 1, BT), F32),
            pltpu.VMEM((G, 1, BT), F32),
            pltpu.VMEM((G, 1, BT), F32),
            pltpu.VMEM((2, 2, FAR, BT, HD), BF16),
            pltpu.VMEM((2, 2, FAR, BT, HD), BF16),
            pltpu.VMEM((2, 2, ND, BT, HD), F32),
            pltpu.VMEM((2, 2, BT, HD), BF16),
            pltpu.VMEM((BT, 2 * G * HD), BF16),
            pltpu.VMEM((2, 1, 128), jnp.int32),
            dma((2, 2, ND, 2)), dma((2, 2, 2)), dma((2, 2, FAR - 1, 2)), dma((2, 2)), dma((2, 2)),
            dma((2, 2)), dma((2, 2)), dma((2, 2)), dma, dma,
            dma((2, 2, FAR, 2)), dma((2, 2, FAR, 2)), dma((2,)), dma((2,)), dma((2,)),
            dma((2, 2)), dma((2, 2)), dma((2, 2)),
        ],
        compiler_params=pltpu.CompilerParams(
            collective_id=0, has_side_effects=True, vmem_limit_bytes=58 * 1024 * 1024
        ),
    )(
        queries, keys, values, segments.reshape(devices, 128),
        loss_mask.reshape(1, 128), grad_out,
    )


def solution(mesh):
    tokens = P(("dp", "cp"), None)
    placed = (tokens, tokens, tokens, P("dp"), P(("dp", "cp")), tokens)
    return jax.shard_map(
        per_device, mesh=mesh, in_specs=placed, out_specs=(tokens, tokens, tokens),
        check_vma=False,
    )
```

```python
import functools
import math

import jax
import jax.numpy as jnp
from jax import lax
from jax.experimental import pallas as pl
from jax.experimental.pallas import tpu as pltpu
from jax.sharding import PartitionSpec as P

HD = 128
BT = 256
ND = 5
G = 8
FAR = ND - 1
NEG = -1e30
U1 = 4
U2 = 8
U3 = 4
F32 = jnp.float32
BF16 = jnp.bfloat16
MESH = pl.DeviceIdType.MESH


def dot(a, b, ca, cb):
    return lax.dot_general(
        a, b, (((ca,), (cb,)), ((), ())), preferred_element_type=F32
    )


def kernel(
    chips, q_hbm, k_hbm, v_hbm, seg_hbm, mask_hbm, do_hbm,
    dq_out, gk_out, gv_out,
    q_s, o_s, kv_s, bias_s, e_s, dp_s, ds_s, p_s, kt_s, m_s, l_s, dl_s,
    rbuf, sbuf, gacc, gout, dq_s, mk_s, seg_ref,
    f_recv, f_own, f_relay, f_xsend, f_loc,
    q_recv, q_send, q_loc, k_recv, k_send, s_loc,
    b_recv, b_send, dq_recv, dq_send, dq_loc, g_recv, g_send, g_loc,
):
    me = lax.axis_index("cp")
    core = me % 2
    chip = me // 2
    other = 1 - core
    partner = chip * 2 + other
    after = (chip + 1) % chips
    before = (chip + chips - 1) % chips
    scale = HD ** -0.5
    mine = pl.ds(pl.multiple_of(core * 128, 128), 128)
    theirs = pl.ds(pl.multiple_of(other * 128, 128), 128)

    barrier = pltpu.get_barrier_semaphore()
    for peer in (partner, after * 2, after * 2 + 1, before * 2, before * 2 + 1):
        pl.semaphore_signal(barrier, inc=1, device_id={"cp": peer}, device_id_type=MESH)

    def remote(src, dst, ssem, rsem, cp):
        return pltpu.make_async_remote_copy(
            src_ref=src, dst_ref=dst, send_sem=ssem, recv_sem=rsem,
            device_id={"cp": cp}, device_id_type=MESH,
        )

    def columns(first, count=1):
        return pl.ds(pl.multiple_of(first * 128, 128), count * 128)

    srcs = (k_hbm, v_hbm)

    def own_send(hl, kv, b):
        return remote(
            srcs[kv].at[:, columns(2 * b + hl)], kv_s.at[hl, kv, 1, mine, :],
            f_own.at[hl, kv, b], f_recv.at[hl, kv, 1, core], after * 2 + b,
        )

    def x_send(hl, kv):
        return remote(
            srcs[kv].at[:, columns(2 * other + hl)], kv_s.at[hl, kv, 0, mine, :],
            f_xsend.at[hl, kv], f_recv.at[hl, kv, 0, core], partner,
        )

    def x_recv(hl, kv):
        return remote(
            srcs[kv].at[:, columns(2 * other + hl)], kv_s.at[hl, kv, 0, theirs, :],
            f_xsend.at[hl, kv], f_recv.at[hl, kv, 0, other], partner,
        )

    def local_kv(hl, kv):
        return pltpu.make_async_copy(
            srcs[kv].at[:, columns(2 * core + hl)], kv_s.at[hl, kv, 0, mine, :],
            f_loc.at[hl, kv],
        )

    def half(i):
        return pl.ds(i * 128, 128)

    def hop(hl, kv, d, i):
        return remote(
            kv_s.at[hl, kv, d, half(i), :], kv_s.at[hl, kv, d + 1, half(i), :],
            f_relay.at[hl, kv, d - 1, i], f_recv.at[hl, kv, d + 1, i],
            after * 2 + core,
        )

    def hop_recv(hl, kv, d, i):
        return remote(
            kv_s.at[hl, kv, d, half(i), :], kv_s.at[hl, kv, d, half(i), :],
            f_relay.at[hl, kv, 0, i], f_recv.at[hl, kv, d, i],
            after * 2 + core,
        )

    heads = (q_hbm, do_hbm)
    held = (q_s, o_s)

    def qo_send(t, i):
        hl = i // G
        return remote(
            heads[t].at[:, columns(other * 16 + i)], held[t].at[i, mine, :],
            q_send.at[t, hl], q_recv.at[t, hl], partner,
        )

    def qo_local(t, i):
        return pltpu.make_async_copy(
            heads[t].at[:, columns(core * 16 + i)], held[t].at[i, mine, :],
            q_loc.at[t, i // G],
        )

    def qo_wait(t, hl):
        rows = held[t].at[hl * G:(hl + 1) * G, theirs, :]
        remote(rows, rows, q_send.at[t, hl], q_recv.at[t, hl], partner).wait_recv()
        own = held[t].at[hl * G:(hl + 1) * G, mine, :]
        pltpu.make_async_copy(own, own, q_loc.at[t, hl]).wait()

    def qo_wait_send(t, hl):
        rows = held[t].at[hl * G:(hl + 1) * G, theirs, :]
        remote(rows, rows, q_send.at[t, hl], q_recv.at[t, hl], partner).wait_send()

    mask_copy = remote(mask_hbm, mk_s.at[core], k_send, k_recv, partner)
    mask_back = remote(mask_hbm, mk_s.at[other], k_send, k_recv, partner)

    seg_copy = pltpu.make_async_copy(seg_hbm, seg_ref, s_loc.at[0])
    mask_own = pltpu.make_async_copy(mask_hbm, mk_s.at[core], s_loc.at[1])
    seg_copy.start()
    mask_own.start()
    for kv in range(2):
        local_kv(0, kv).start()
    for t in range(2):
        for i in range(G):
            qo_local(t, i).start()
    seg_copy.wait()

    first = 2 * chip - 2 * FAR

    def seg_row(j):
        return seg_ref[pl.ds((first + j + 2 * chips) % (2 * chips), 1), :].astype(F32)

    q_seg = jnp.concatenate([seg_row(2 * FAR), seg_row(2 * FAR + 1)], axis=1)
    q_at = lax.broadcasted_iota(jnp.int32, (128, BT), 1)
    k_at = lax.broadcasted_iota(jnp.int32, (128, BT), 0)
    for j in range(2 * ND):
        row = jnp.broadcast_to(seg_row(j), (128, 128))
        col = jnp.concatenate([row.T] * 2, axis=1)
        offset = (j - 2 * FAR) * 128
        ok = (col == q_seg) & (k_at + offset <= q_at) & (k_at + (first + j) * 128 >= 0)
        bias_s[FAR - j // 2, (j % 2) * 128:(j % 2) * 128 + 128, :] = jnp.where(ok, 0.0, NEG)

    pl.semaphore_wait(barrier, 5)
    for kv in range(2):
        for b in range(2):
            own_send(0, kv, b).start()
    for kv in range(2):
        x_send(0, kv).start()
    mask_copy.start()
    for t in range(2):
        for i in range(G):
            qo_send(t, i).start()
    mask_own.wait()
    mask_back.wait_recv()
    mask_col = jnp.concatenate(
        [jnp.broadcast_to(mk_s[i].astype(F32), (128, 128)).T for i in range(2)], axis=0
    ).astype(BF16)

    def mask_grad(hl):
        def body(i, carry):
            o_s[hl * G + i] = o_s[hl * G + i] * mask_col
            return carry
        lax.fori_loop(0, G, body, 0)

    def arrive(hl, d):
        for kv in range(2):
            if d == 0:
                local_kv(hl, kv).wait()
                x_recv(hl, kv).wait_recv()
            else:
                for i in range(2):
                    hop_recv(hl, kv, d, i).wait_recv()
                    if d < FAR:
                        hop(hl, kv, d, i).start()

    c2 = scale * math.log2(math.e)

    def by_eight(x):
        return x.reshape(BT // 8, 8, BT)

    def pass1(hl, d):
        def body(g, carry):
            s = dot(kv_s[hl, 0, d], q_s[hl * G + g], 1, 1)
            dp = dot(kv_s[hl, 1, d], o_s[hl * G + g], 1, 1)
            x = by_eight(s * c2 + bias_s[d])
            dp = by_eight(dp)
            peak = jnp.max(x, axis=0)
            if d > 0:
                old = m_s[d - 1, g]
                peak = jnp.maximum(old, peak)
            e = jnp.exp2(x - peak[None])
            total = jnp.sum(e, axis=0)
            inner = jnp.sum(e * dp, axis=0)
            if d > 0:
                fade = jnp.exp2(old - peak)
                total = total + l_s[g] * fade
                inner = inner + dl_s[g] * fade
            m_s[d, g] = peak
            l_s[g] = total
            dl_s[g] = inner
            e_s[g, d] = e.reshape(BT, BT)
            dp_s[g, d] = dp.reshape(BT, BT)
            return carry
        lax.fori_loop(0, G, body, 0, unroll=U1)

    def settle():
        def body(g, carry):
            peak = m_s[FAR, g]
            top = jnp.broadcast_to(jnp.max(peak, axis=0, keepdims=True), (8, BT))
            fade = jnp.exp2(peak - top)
            total = jnp.sum(l_s[g] * fade, axis=0, keepdims=True)
            inner = jnp.sum(dl_s[g] * fade, axis=0, keepdims=True)
            inv = 1.0 / total
            dl_s[g] = jnp.broadcast_to(inner * inv, (8, BT))
            inv = jnp.broadcast_to(inv, (8, BT))
            for d in range(ND):
                m_s[d, g] = jnp.exp2(m_s[d, g] - top) * inv
            return carry
        lax.fori_loop(0, G, body, 0)

    def pass2(hl, d):
        span = slice(d * BT, (d + 1) * BT)
        def body(g, carry):
            p = by_eight(e_s[g, d]) * m_s[d, g][None]
            ds = p * (by_eight(dp_s[g, d]) - dl_s[g][None])
            p_s[g] = p.reshape(BT, BT).astype(BF16)
            ds_s[hl * G + g, span, :] = ds.reshape(BT, BT).astype(BF16)
            return carry
        lax.fori_loop(0, G, body, 0, unroll=U2)
        span = slice(hl * G, (hl + 1) * G)
        ds = jnp.concatenate([ds_s[hl * G + g, d * BT:(d + 1) * BT, :] for g in range(G)], axis=1)
        gacc[hl, 0, d] = dot(ds, q_s[span].reshape(G * BT, HD), 1, 0)
        p = jnp.concatenate([p_s[g] for g in range(G)], axis=1)
        gacc[hl, 1, d] = dot(p, o_s[span].reshape(G * BT, HD), 1, 0)

    def transposed_keys(hl):
        for d in range(ND):
            kt_s[:, d * BT:(d + 1) * BT] = kv_s[hl, 0, d].astype(F32).T.astype(BF16)

    def grad_q(hl):
        def body(g, carry):
            dqt = dot(kt_s[...], ds_s[hl * G + g], 1, 0) * scale
            dq_s[:, columns(hl * G + g)] = dqt.T.astype(BF16)
            return carry
        lax.fori_loop(0, G, body, 0, unroll=U3)

    def dq_copy(hl):
        return pltpu.make_async_copy(
            dq_s.at[mine, columns(hl * G, G)],
            dq_out.at[:, columns(core * 16 + hl * G, G)], dq_loc.at[hl],
        )

    def dq_give(hl):
        return remote(
            dq_s.at[theirs, columns(hl * G, G)],
            dq_out.at[:, columns(core * 16 + hl * G, G)],
            dq_send.at[hl], dq_recv.at[hl], partner,
        )

    def dq_take(hl):
        return remote(
            dq_s.at[theirs, columns(hl * G, G)],
            dq_out.at[:, columns(other * 16 + hl * G, G)],
            dq_send.at[hl], dq_recv.at[hl], partner,
        )

    def back(hl, kv, d, i):
        return remote(
            sbuf.at[hl, kv, d - 1, half(i), :], rbuf.at[hl, kv, d - 1, half(i), :],
            b_send.at[hl, kv, d - 1, i], b_recv.at[hl, kv, d - 1, i],
            before * 2 + core,
        )

    outs = (gk_out, gv_out)

    def g_copy(hl, kv):
        return pltpu.make_async_copy(
            gout.at[hl, kv, mine, :], outs[kv].at[:, columns(2 * core + hl)],
            g_loc.at[hl, kv],
        )

    def g_give(hl, kv):
        return remote(
            gout.at[hl, kv, theirs, :], outs[kv].at[:, columns(2 * core + hl)],
            g_send.at[hl, kv], g_recv.at[hl, kv], partner,
        )

    def g_take(hl, kv):
        return remote(
            gout.at[hl, kv, theirs, :], outs[kv].at[:, columns(2 * other + hl)],
            g_send.at[hl, kv], g_recv.at[hl, kv], partner,
        )

    def chain(hl, d):
        for kv in range(2):
            for i in range(2):
                rows = slice(i * 128, i * 128 + 128)
                part = gacc[hl, kv, d, rows, :]
                if d < FAR:
                    back(hl, kv, d + 1, i).wait_recv()
                    part = part + rbuf[hl, kv, d, rows, :].astype(F32)
                if d > 0:
                    sbuf[hl, kv, d - 1, rows, :] = part.astype(BF16)
                    back(hl, kv, d, i).start()
                else:
                    if kv == 0:
                        part = part * scale
                    gout[hl, kv, rows, :] = part.astype(BF16)
            if d == 0:
                g_give(hl, kv).start()
                g_copy(hl, kv).start()

    def start_second():
        for kv in range(2):
            for b in range(2):
                own_send(1, kv, b).start()
        for kv in range(2):
            x_send(1, kv).start()
            local_kv(1, kv).start()
        for t in range(2):
            for i in range(G, 2 * G):
                qo_send(t, i).start()
                qo_local(t, i).start()

    qo_wait(0, 0)
    qo_wait(1, 0)
    mask_grad(0)
    for d in range(ND):
        arrive(0, d)
        if d == FAR - 1:
            start_second()
        pass1(0, d)
    settle()
    pass2(0, 4)
    chain(0, 4)
    arrive(1, 0)
    arrive(1, 1)
    pass2(0, 3)
    pass2(0, 2)
    pass2(0, 1)
    chain(0, 3)
    arrive(1, 2)
    pass2(0, 0)
    qo_wait(0, 1)
    qo_wait(1, 1)
    mask_grad(1)
    pass1(1, 0)
    pass1(1, 1)
    chain(0, 2)
    arrive(1, 3)
    pass1(1, 2)
    pass1(1, 3)
    chain(0, 1)
    arrive(1, 4)
    pass1(1, 4)
    settle()
    pass2(1, 4)
    chain(1, 4)
    chain(0, 0)
    pass2(1, 3)
    pass2(1, 2)
    chain(1, 3)
    pass2(1, 1)
    pass2(1, 0)
    transposed_keys(0)
    grad_q(0)
    dq_give(0).start()
    dq_copy(0).start()
    chain(1, 2)
    transposed_keys(1)
    grad_q(1)
    dq_give(1).start()
    dq_copy(1).start()
    chain(1, 1)
    chain(1, 0)

    mask_copy.wait_send()
    for hl in range(2):
        for t in range(2):
            qo_wait_send(t, hl)
        dq_give(hl).wait_send()
        dq_copy(hl).wait()
        for kv in range(2):
            for b in range(2):
                own_send(hl, kv, b).wait_send()
            x_send(hl, kv).wait_send()
            for i in range(2):
                for d in range(1, FAR):
                    hop(hl, kv, d, i).wait_send()
                for d in range(1, ND):
                    back(hl, kv, d, i).wait_send()
            g_give(hl, kv).wait_send()
            g_copy(hl, kv).wait()
    for hl in range(2):
        dq_take(hl).wait_recv()
        for kv in range(2):
            g_take(hl, kv).wait_recv()


def per_device(queries, keys, values, segments, loss_mask, grad_out):
    devices = lax.axis_size("cp")
    chips = devices // 2
    dma = pltpu.SemaphoreType.DMA
    hbm = pl.BlockSpec(memory_space=pltpu.HBM)
    vmem = pl.BlockSpec(memory_space=pltpu.VMEM)
    return pl.pallas_call(
        functools.partial(kernel, chips),
        out_shape=(
            pltpu.VMEM(queries.shape, BF16),
            pltpu.VMEM(keys.shape, BF16),
            pltpu.VMEM(values.shape, BF16),
        ),
        in_specs=[hbm] * 6,
        out_specs=(vmem, vmem, vmem),
        scratch_shapes=[
            pltpu.VMEM((2 * G, BT, HD), BF16),
            pltpu.VMEM((2 * G, BT, HD), BF16),
            pltpu.VMEM((2, 2, ND, BT, HD), BF16),
            pltpu.VMEM((ND, BT, BT), F32),
            pltpu.VMEM((G, ND, BT, BT), F32),
            pltpu.VMEM((G, ND, BT, BT), F32),
            pltpu.VMEM((2 * G, ND * BT, BT), BF16),
            pltpu.VMEM((G, BT, BT), BF16),
            pltpu.VMEM((HD, ND * BT), BF16),
            pltpu.VMEM((ND, G, 8, BT), F32),
            pltpu.VMEM((G, 8, BT), F32),
            pltpu.VMEM((G, 8, BT), F32),
            pltpu.VMEM((2, 2, FAR, BT, HD), BF16),
            pltpu.VMEM((2, 2, FAR, BT, HD), BF16),
            pltpu.VMEM((2, 2, ND, BT, HD), F32),
            pltpu.VMEM((2, 2, BT, HD), BF16),
            pltpu.VMEM((BT, 2 * G * HD), BF16),
            pltpu.VMEM((2, 1, 128), jnp.int32),
            pltpu.VMEM((devices, 128), jnp.int32),
            dma((2, 2, ND, 2)), dma((2, 2, 2)), dma((2, 2, FAR - 1, 2)), dma((2, 2)), dma((2, 2)),
            dma((2, 2)), dma((2, 2)), dma((2, 2)), dma, dma, dma((2,)),
            dma((2, 2, FAR, 2)), dma((2, 2, FAR, 2)), dma((2,)), dma((2,)), dma((2,)),
            dma((2, 2)), dma((2, 2)), dma((2, 2)),
        ],
        compiler_params=pltpu.CompilerParams(
            collective_id=0, has_side_effects=True, vmem_limit_bytes=56 * 1024 * 1024
        ),
    )(
        queries, keys, values, segments.reshape(devices, 128),
        loss_mask.reshape(1, 128), grad_out,
    )


def solution(mesh):
    tokens = P(("dp", "cp"), None)
    placed = (tokens, tokens, tokens, P("dp"), P(("dp", "cp")), tokens)
    return jax.shard_map(
        per_device, mesh=mesh, in_specs=placed, out_specs=(tokens, tokens, tokens),
        check_vma=False,
    )
```

```python
import functools
import math

import jax
import jax.numpy as jnp
from jax import lax
from jax.experimental import pallas as pl
from jax.experimental.pallas import tpu as pltpu
from jax.sharding import PartitionSpec as P

HD = 128
BT = 256
ND = 5
G = 8
FAR = ND - 1
SIDE = 8
NEG = -1e30
U1 = 4
U2 = 8
U3 = 4
F32 = jnp.float32
BF16 = jnp.bfloat16
MESH = pl.DeviceIdType.MESH


def dot(a, b, ca, cb):
    return lax.dot_general(
        a, b, (((ca,), (cb,)), ((), ())), preferred_element_type=F32
    )


def kernel(
    chips, q_hbm, k_hbm, v_hbm, seg_hbm, mask_hbm, do_hbm,
    out,
    q_s, o_s, kv_s, bias_s, e_s, dp_s, ds_s, p_s, kt_s, m_s, l_s, dl_s,
    rbuf, sbuf, gacc, xsend, xback, rlast, mbuf, dq_s, mk_s, seg_ref,
    f_recv, f_own, f_relay, f_xsend, f_loc,
    q_recv, q_send, q_loc, k_recv, k_send, s_loc,
    b_recv, b_send, dq_recv, dq_send, dq_loc, g_recv, g_send, l_recv,
    m_recv, m_own, m_relay,
):
    me = lax.axis_index("cp")
    core = me % 2
    chip = me // 2
    other = 1 - core
    partner = chip * 2 + other
    after = (chip + 1) % chips
    before = (chip + chips - 1) % chips
    scale = HD ** -0.5

    def along(who, steps):
        return who // SIDE * SIDE + (who % SIDE + steps) % SIDE

    mid_to = along(chip, SIDE - 2)
    mid_from = along(chip, 2)
    far_to = (mid_from + FAR) % chips
    far_from = along((chip + chips - FAR) % chips, SIDE - 2)
    mine = pl.ds(pl.multiple_of(core * 128, 128), 128)
    theirs = pl.ds(pl.multiple_of(other * 128, 128), 128)

    barrier = pltpu.get_barrier_semaphore()
    for peer in (
        partner, after * 2, after * 2 + 1, before * 2, before * 2 + 1,
    ):
        pl.semaphore_signal(barrier, inc=1, device_id={"cp": peer}, device_id_type=MESH)

    def remote(src, dst, ssem, rsem, cp):
        return pltpu.make_async_remote_copy(
            src_ref=src, dst_ref=dst, send_sem=ssem, recv_sem=rsem,
            device_id={"cp": cp}, device_id_type=MESH,
        )

    def columns(first, count=1):
        return pl.ds(pl.multiple_of(first * 128, 128), count * 128)

    srcs = (k_hbm, v_hbm)

    def own_send(hl, kv, b):
        return remote(
            srcs[kv].at[:, columns(2 * b + hl)], kv_s.at[hl, kv, 1, mine, :],
            f_own.at[hl, kv, b], f_recv.at[hl, kv, 1, core], after * 2 + b,
        )

    def mid_send(kv, b):
        return remote(
            srcs[kv].at[:, columns(2 * b)], mbuf.at[kv, mine, :],
            m_own.at[kv, b], m_recv.at[kv, core], mid_to * 2 + b,
        )

    def mid_recv(kv, i):
        return remote(
            mbuf.at[kv, half(i), :], mbuf.at[kv, half(i), :],
            m_relay.at[kv, i], m_recv.at[kv, i], mid_to * 2,
        )

    def mid_hop(kv, i):
        return remote(
            mbuf.at[kv, half(i), :], kv_s.at[0, kv, FAR, half(i), :],
            m_relay.at[kv, i], f_recv.at[0, kv, FAR, i], far_to * 2 + core,
        )

    def pass_far():
        for i in range(2):
            mid_recv(0, i).wait_recv()
            mid_hop(0, i).start()

    def goes_on(hl, kv, d):
        return d < FAR

    def x_send(hl, kv):
        return remote(
            srcs[kv].at[:, columns(2 * other + hl)], kv_s.at[hl, kv, 0, mine, :],
            f_xsend.at[hl, kv], f_recv.at[hl, kv, 0, core], partner,
        )

    def x_recv(hl, kv):
        return remote(
            srcs[kv].at[:, columns(2 * other + hl)], kv_s.at[hl, kv, 0, theirs, :],
            f_xsend.at[hl, kv], f_recv.at[hl, kv, 0, other], partner,
        )

    def local_kv(hl, kv):
        return pltpu.make_async_copy(
            srcs[kv].at[:, columns(2 * core + hl)], kv_s.at[hl, kv, 0, mine, :],
            f_loc.at[hl, kv],
        )

    def half(i):
        return pl.ds(i * 128, 128)

    def hop(hl, kv, d, i):
        return remote(
            kv_s.at[hl, kv, d, half(i), :], kv_s.at[hl, kv, d + 1, half(i), :],
            f_relay.at[hl, kv, d - 1, i], f_recv.at[hl, kv, d + 1, i],
            after * 2 + core,
        )

    def hop_recv(hl, kv, d, i):
        return remote(
            kv_s.at[hl, kv, d, half(i), :], kv_s.at[hl, kv, d, half(i), :],
            f_relay.at[hl, kv, 0, i], f_recv.at[hl, kv, d, i],
            after * 2 + core,
        )

    heads = (q_hbm, do_hbm)
    held = (q_s, o_s)

    def qo_send(t, i):
        hl = i // G
        return remote(
            heads[t].at[:, columns(other * 16 + i)], held[t].at[i, mine, :],
            q_send.at[t, hl], q_recv.at[t, hl], partner,
        )

    def qo_local(t, i):
        return pltpu.make_async_copy(
            heads[t].at[:, columns(core * 16 + i)], held[t].at[i, mine, :],
            q_loc.at[t, i // G],
        )

    def qo_wait(t, hl):
        rows = held[t].at[hl * G:(hl + 1) * G, theirs, :]
        remote(rows, rows, q_send.at[t, hl], q_recv.at[t, hl], partner).wait_recv()
        own = held[t].at[hl * G:(hl + 1) * G, mine, :]
        pltpu.make_async_copy(own, own, q_loc.at[t, hl]).wait()

    def qo_wait_send(t, hl):
        rows = held[t].at[hl * G:(hl + 1) * G, theirs, :]
        remote(rows, rows, q_send.at[t, hl], q_recv.at[t, hl], partner).wait_send()

    mask_copy = remote(mask_hbm, mk_s.at[core], k_send, k_recv, partner)
    mask_back = remote(mask_hbm, mk_s.at[other], k_send, k_recv, partner)

    seg_copy = pltpu.make_async_copy(seg_hbm, seg_ref, s_loc.at[0])
    mask_own = pltpu.make_async_copy(mask_hbm, mk_s.at[core], s_loc.at[1])
    seg_copy.start()
    mask_own.start()
    for kv in range(2):
        local_kv(0, kv).start()
    for t in range(2):
        for i in range(G):
            qo_local(t, i).start()
    seg_copy.wait()

    first = 2 * chip - 2 * FAR

    def seg_row(j):
        return seg_ref[pl.ds((first + j + 2 * chips) % (2 * chips), 1), :].astype(F32)

    q_seg = jnp.concatenate([seg_row(2 * FAR), seg_row(2 * FAR + 1)], axis=1)
    q_at = lax.broadcasted_iota(jnp.int32, (128, BT), 1)
    k_at = lax.broadcasted_iota(jnp.int32, (128, BT), 0)
    for j in range(2 * ND):
        row = jnp.broadcast_to(seg_row(j), (128, 128))
        col = jnp.concatenate([row.T] * 2, axis=1)
        offset = (j - 2 * FAR) * 128
        ok = (col == q_seg) & (k_at + offset <= q_at) & (k_at + (first + j) * 128 >= 0)
        bias_s[FAR - j // 2, (j % 2) * 128:(j % 2) * 128 + 128, :] = jnp.where(ok, 0.0, NEG)

    pl.semaphore_wait(barrier, 5)
    for kv in range(2):
        for b in range(2):
            own_send(0, kv, b).start()
    for kv in range(2):
        x_send(0, kv).start()
    mask_copy.start()
    for t in range(2):
        for i in range(G):
            qo_send(t, i).start()
    mask_own.wait()
    mask_back.wait_recv()
    mask_col = jnp.concatenate(
        [jnp.broadcast_to(mk_s[i].astype(F32), (128, 128)).T for i in range(2)], axis=0
    ).astype(BF16)

    def mask_grad(hl):
        def body(i, carry):
            o_s[hl * G + i] = o_s[hl * G + i] * mask_col
            return carry
        lax.fori_loop(0, G, body, 0)

    def arrive(hl, d, kvs=(0, 1)):
        for kv in kvs:
            if d == 0:
                local_kv(hl, kv).wait()
                x_recv(hl, kv).wait_recv()
            else:
                for i in range(2):
                    hop_recv(hl, kv, d, i).wait_recv()
                    if goes_on(hl, kv, d):
                        hop(hl, kv, d, i).start()

    c2 = scale * math.log2(math.e)

    def by_eight(x):
        return x.reshape(BT // 8, 8, BT)

    def slot(hl, d):
        if hl == 0:
            return d
        return ND if d == FAR else FAR - d

    def pass1(hl, d):
        def body(g, carry):
            s = dot(kv_s[hl, 0, d], q_s[hl * G + g], 1, 1)
            dp = dot(kv_s[hl, 1, d], o_s[hl * G + g], 1, 1)
            x = by_eight(s * c2 + bias_s[d])
            dp = by_eight(dp)
            peak = jnp.max(x, axis=0)
            if d > 0:
                old = m_s[hl, d - 1, g]
                peak = jnp.maximum(old, peak)
            e = jnp.exp2(x - peak[None])
            total = jnp.sum(e, axis=0)
            inner = jnp.sum(e * dp, axis=0)
            if d > 0:
                fade = jnp.exp2(old - peak)
                total = total + l_s[hl, g] * fade
                inner = inner + dl_s[hl, g] * fade
            m_s[hl, d, g] = peak
            l_s[hl, g] = total
            dl_s[hl, g] = inner
            e_s[g, slot(hl, d)] = e.reshape(BT, BT)
            dp_s[g, slot(hl, d)] = dp.reshape(BT, BT)
            return carry
        lax.fori_loop(0, G, body, 0, unroll=U1)

    def scores_only(hl):
        def body(g, carry):
            s = dot(kv_s[hl, 0, FAR], q_s[hl * G + g], 1, 1)
            x = by_eight(s * c2 + bias_s[FAR])
            old = m_s[hl, FAR - 1, g]
            peak = jnp.maximum(old, jnp.max(x, axis=0))
            e = jnp.exp2(x - peak[None])
            fade = jnp.exp2(old - peak)
            l_s[hl, g] = jnp.sum(e, axis=0) + l_s[hl, g] * fade
            dl_s[hl, g] = dl_s[hl, g] * fade
            m_s[hl, FAR, g] = peak
            e_s[g, slot(hl, FAR)] = e.reshape(BT, BT)
            return carry
        lax.fori_loop(0, G, body, 0, unroll=U1)

    def dprobs_only(hl):
        def body(g, carry):
            dp = by_eight(dot(kv_s[hl, 1, FAR], o_s[hl * G + g], 1, 1))
            inner = jnp.sum(by_eight(e_s[g, slot(hl, FAR)]) * dp, axis=0) + dl_s[hl, g]
            delta = jnp.sum(inner * m_s[hl, FAR, g], axis=0, keepdims=True)
            dl_s[hl, g] = jnp.broadcast_to(delta, (8, BT))
            dp_s[g, slot(hl, FAR)] = dp.reshape(BT, BT)
            return carry
        lax.fori_loop(0, G, body, 0, unroll=U1)

    def settle(hl, delta=True):
        def body(g, carry):
            peak = m_s[hl, FAR, g]
            top = jnp.broadcast_to(jnp.max(peak, axis=0, keepdims=True), (8, BT))
            fade = jnp.exp2(peak - top)
            total = jnp.sum(l_s[hl, g] * fade, axis=0, keepdims=True)
            inv = 1.0 / total
            if delta:
                inner = jnp.sum(dl_s[hl, g] * fade, axis=0, keepdims=True)
                dl_s[hl, g] = jnp.broadcast_to(inner * inv, (8, BT))
            inv = jnp.broadcast_to(inv, (8, BT))
            for d in range(ND):
                m_s[hl, d, g] = jnp.exp2(m_s[hl, d, g] - top) * inv
            return carry
        lax.fori_loop(0, G, body, 0)

    def pass2(hl, d, kvs=(0, 1)):
        keys = slice(d * BT, (d + 1) * BT)
        def body(g, carry):
            p = by_eight(e_s[g, slot(hl, d)]) * m_s[hl, d, g][None]
            if 1 in kvs:
                p_s[g] = p.reshape(BT, BT).astype(BF16)
            if 0 in kvs:
                ds = p * (by_eight(dp_s[g, slot(hl, d)]) - dl_s[hl, g][None])
                ds_s[hl * G + g, keys, :] = ds.reshape(BT, BT).astype(BF16)
            return carry
        lax.fori_loop(0, G, body, 0, unroll=U2)
        span = slice(hl * G, (hl + 1) * G)
        if 0 in kvs:
            ds = jnp.concatenate([ds_s[hl * G + g, keys, :] for g in range(G)], axis=1)
            gacc[hl, 0, d] = dot(ds, q_s[span].reshape(G * BT, HD), 1, 0)
        if 1 in kvs:
            p = jnp.concatenate([p_s[g] for g in range(G)], axis=1)
            gacc[hl, 1, d] = dot(p, o_s[span].reshape(G * BT, HD), 1, 0)

    def transposed_keys(hl):
        for d in range(ND):
            kt_s[:, d * BT:(d + 1) * BT] = kv_s[hl, 0, d].astype(F32).T.astype(BF16)

    def grad_q(hl):
        def body(g, carry):
            dqt = dot(kt_s[...], ds_s[hl * G + g], 1, 0) * scale
            dq_s[:, columns(hl * G + g)] = dqt.T.astype(BF16)
            out[:, columns(core * 16 + hl * G + g)] = dq_s[mine, columns(hl * G + g)]
            return carry
        lax.fori_loop(0, G, body, 0, unroll=U3)

    def dq_give(hl):
        return remote(
            dq_s.at[theirs, columns(hl * G, G)],
            out.at[:, columns(core * 16 + hl * G, G)],
            dq_send.at[hl], dq_recv.at[hl], partner,
        )

    def dq_take(hl):
        return remote(
            dq_s.at[theirs, columns(hl * G, G)],
            out.at[:, columns(other * 16 + hl * G, G)],
            dq_send.at[hl], dq_recv.at[hl], partner,
        )

    def back(hl, kv, d, i):
        return remote(
            sbuf.at[hl, kv, d - 1, half(i), :], rbuf.at[hl, kv, d - 1, half(i), :],
            b_send.at[hl, kv, d - 1, i], b_recv.at[hl, kv, d - 1, i],
            before * 2 + core,
        )

    def last(hl, kv, i):
        return remote(
            sbuf.at[hl, kv, 0, half(i), :], rlast.at[hl, kv, core],
            b_send.at[hl, kv, 0, i], l_recv.at[hl, kv, core], before * 2 + i,
        )

    def last_recv(hl, kv, i):
        return remote(
            sbuf.at[hl, kv, 0, half(i), :], rlast.at[hl, kv, i],
            b_send.at[hl, kv, 0, i], l_recv.at[hl, kv, i], before * 2 + i,
        )

    def g_give(hl, kv):
        return remote(
            xsend.at[hl, kv], xback.at[hl, kv],
            g_send.at[hl, kv], g_recv.at[hl, kv], partner,
        )

    def own_block(hl):
        for kv in range(2):
            xsend[hl, kv] = gacc[hl, kv, 0, theirs, :].astype(BF16)
            g_give(hl, kv).start()

    def link(hl, d, kv, i):
        rows = slice(i * 128, i * 128 + 128)
        part = gacc[hl, kv, d, rows, :]
        if d < FAR:
            back(hl, kv, d + 1, i).wait_recv()
            part = part + rbuf[hl, kv, d, rows, :].astype(F32)
        sbuf[hl, kv, d - 1, rows, :] = part.astype(BF16)
        if d > 1:
            back(hl, kv, d, i).start()
        else:
            last(hl, kv, i).start()

    def chain(hl, d, kvs=(1, 0)):
        for kv in kvs:
            for i in range(2):
                link(hl, d, kv, i)

    def finish(hl, kv):
        factor = scale if kv == 0 else 1.0
        g_give(hl, kv).wait_recv()
        for i in range(2):
            last_recv(hl, kv, i).wait_recv()
        part = gacc[hl, kv, 0, mine, :] + rlast[hl, kv, core].astype(F32)
        out[:, columns(32 + 4 * kv + 2 * core + hl)] = (part * factor).astype(BF16)
        part = xback[hl, kv].astype(F32) + rlast[hl, kv, other].astype(F32)
        out[:, columns(32 + 4 * kv + 2 * other + hl)] = (part * factor).astype(BF16)

    def start_second():
        for kv in range(2):
            x_send(1, kv).start()
            local_kv(1, kv).start()
        for t in range(2):
            for i in range(G, 2 * G):
                qo_send(t, i).start()
                qo_local(t, i).start()

    qo_wait(0, 0)
    qo_wait(1, 0)
    mask_grad(0)
    arrive(0, 0)
    pass1(0, 0)
    arrive(0, 1)
    pass1(0, 1)
    arrive(0, 2)
    pass1(0, 2)
    arrive(0, 3)
    own_send(1, 0, 0).start()
    own_send(1, 0, 1).start()
    own_send(1, 1, 0).start()
    own_send(1, 1, 1).start()
    start_second()
    pass1(0, 3)
    arrive(0, 4)
    pass1(0, 4)
    arrive(1, 1)
    settle(0)
    pass2(0, 4)
    chain(0, 4)
    pass2(0, 3)
    arrive(1, 2)
    pass2(0, 2)
    pass2(0, 1)
    chain(0, 3)
    arrive(1, 0)
    arrive(1, 3)
    qo_wait(0, 1)
    qo_wait(1, 1)
    mask_grad(1)
    pass1(1, 0)
    pass1(1, 1)
    chain(0, 2)
    pass1(1, 2)
    pass1(1, 3)
    arrive(1, 4, (0,))
    scores_only(1)
    settle(1, False)
    pass2(1, 4, (1,))
    chain(1, 4, (1,))
    arrive(1, 4, (1,))
    link(0, 1, 1, 0)
    dprobs_only(1)
    pass2(1, 4, (0,))
    chain(1, 4, (0,))
    link(0, 1, 1, 1)
    pass2(1, 3)
    pass2(0, 0)
    pass2(1, 2)
    chain(1, 3)
    link(0, 1, 0, 0)
    link(0, 1, 0, 1)
    own_block(0)
    transposed_keys(0)
    grad_q(0)
    dq_give(0).start()
    pass2(1, 1)
    chain(1, 2)
    pass2(1, 0)
    own_block(1)
    transposed_keys(1)
    grad_q(1)
    dq_give(1).start()
    chain(1, 1)
    finish(0, 0)
    finish(0, 1)
    mask_copy.wait_send()
    for hl in range(2):
        for t in range(2):
            qo_wait_send(t, hl)
        dq_give(hl).wait_send()
        for kv in range(2):
            for b in range(2):
                own_send(hl, kv, b).wait_send()
            x_send(hl, kv).wait_send()
            for i in range(2):
                for d in range(1, FAR):
                    if goes_on(hl, kv, d):
                        hop(hl, kv, d, i).wait_send()
                for d in range(2, ND):
                    back(hl, kv, d, i).wait_send()
                last(hl, kv, i).wait_send()
            g_give(hl, kv).wait_send()
    for hl in range(2):
        dq_take(hl).wait_recv()
    for kv in (1, 0):
        finish(1, kv)


def per_device(queries, keys, values, segments, loss_mask, grad_out):
    devices = lax.axis_size("cp")
    chips = devices // 2
    dma = pltpu.SemaphoreType.DMA
    hbm = pl.BlockSpec(memory_space=pltpu.HBM)
    vmem = pl.BlockSpec(memory_space=pltpu.VMEM)
    (joined,) = pl.pallas_call(
        functools.partial(kernel, chips),
        out_shape=(
            pltpu.VMEM((queries.shape[0], queries.shape[1] + 2 * keys.shape[1]), BF16),
        ),
        in_specs=[hbm] * 6,
        out_specs=(vmem,),
        scratch_shapes=[
            pltpu.VMEM((2 * G, BT, HD), BF16),
            pltpu.VMEM((2 * G, BT, HD), BF16),
            pltpu.VMEM((2, 2, ND, BT, HD), BF16),
            pltpu.VMEM((ND, BT, BT), F32),
            pltpu.VMEM((G, ND + 1, BT, BT), F32),
            pltpu.VMEM((G, ND + 1, BT, BT), F32),
            pltpu.VMEM((2 * G, ND * BT, BT), BF16),
            pltpu.VMEM((G, BT, BT), BF16),
            pltpu.VMEM((HD, ND * BT), BF16),
            pltpu.VMEM((2, ND, G, 8, BT), F32),
            pltpu.VMEM((2, G, 8, BT), F32),
            pltpu.VMEM((2, G, 8, BT), F32),
            pltpu.VMEM((2, 2, FAR, BT, HD), BF16),
            pltpu.VMEM((2, 2, FAR, BT, HD), BF16),
            pltpu.VMEM((2, 2, ND, BT, HD), F32),
            pltpu.VMEM((2, 2, 128, HD), BF16),
            pltpu.VMEM((2, 2, 128, HD), BF16),
            pltpu.VMEM((2, 2, 2, 128, HD), BF16),
            pltpu.VMEM((1, BT, HD), BF16),
            pltpu.VMEM((BT, 2 * G * HD), BF16),
            pltpu.VMEM((2, 1, 128), jnp.int32),
            pltpu.VMEM((devices, 128), jnp.int32),
            dma((2, 2, ND, 2)), dma((2, 2, 2)), dma((2, 2, FAR - 1, 2)), dma((2, 2)), dma((2, 2)),
            dma((2, 2)), dma((2, 2)), dma((2, 2)), dma, dma, dma((2,)),
            dma((2, 2, FAR, 2)), dma((2, 2, FAR, 2)), dma((2,)), dma((2,)), dma((2,)),
            dma((2, 2)), dma((2, 2)), dma((2, 2, 2)),
            dma((1, 2)), dma((1, 2)), dma((1, 2)),
        ],
        compiler_params=pltpu.CompilerParams(
            collective_id=0, has_side_effects=True, vmem_limit_bytes=56 * 1024 * 1024
        ),
    )(
        queries, keys, values, segments.reshape(devices, 128),
        loss_mask.reshape(1, 128), grad_out,
    )
    wide, narrow = queries.shape[1], keys.shape[1]
    return (
        joined[:, :wide], joined[:, wide:wide + narrow], joined[:, wide + narrow:],
    )


def solution(mesh):
    tokens = P(("dp", "cp"), None)
    placed = (tokens, tokens, tokens, P("dp"), P(("dp", "cp")), tokens)
    return jax.shard_map(
        per_device, mesh=mesh, in_specs=placed, out_specs=(tokens, tokens, tokens),
        check_vma=False,
    )
```
